128 devices in a mesh: narrow: 2 (over core), wide: 64 (over z, y, x).
Axes of the slice: x: 4, y: 4, z: 4, core: 2. Of those that a mesh axis runs over, the one named last changes fastest.
Arguments:
- rows: bfloat16 [393216, 1024], P(('narrow', 'wide')), may hold values from -20 to 20
- list_ids: int32 [393216], P(('narrow', 'wide')), may hold values from 0 to 65535, as said below
- codes: int32 [393216, 64], P(('narrow', 'wide')), may hold values from 0 to 255
- row_counts: int32 [128], P(('narrow', 'wide')), may hold values from 1536 to 3072, as said below
- centroids: bfloat16 [65536, 1024], P('wide'), may hold values from -4 to 4
- old_codebook: float32 [64, 4096], replicated, may hold values from -4 to 4
Outputs:
- codebook: float32 [64, 4096], replicated
- search_table: bfloat16 [64, 4096], P('wide')
- row_error: float32 [393216], P(('narrow', 'wide'))
The draws below stay inside these ranges and needn't reach their ends.
Inputs may be any that keep to these rules, and one draw needn't show every extreme that they name: `list_ids`: among the live passages of one device, at most 96 have lists owned by any one index w of wide (lists w * 1024 to (w + 1) * 1024 - 1), and one index of wide receives exactly 96 live passages from every device. Entries past a device's count are arbitrary. `row_counts`: one device holds exactly 3072 live passages.
All inputs are finite; a program needn't handle non-finite values.
Results may differ from the reference program's by a relative error of at most 0.00165.
Values may be sent and summed in bfloat16 or wider, within the bound.
No kernel may reach another device: no remote copies, remote signals or barrier semaphores. Data moves between devices by JAX's collectives and lax.ppermute only.
A program may use at most 192 MiB of HBM per device.

```python
import jax
import jax.numpy as jnp
from jax import lax

D = 1024
M = 64
K = 256
DSUB = 16
LISTS_DEV = 1024
LISTS = 65536
ROWS_DEV = 3072
ROWS = 393216
CAP = 96
ANCHOR = 384
N_WIDE = 64
DEVICES = 128


def route_plan(key):
    key_count = jax.random.fold_in(key, 1)
    key_full = jax.random.fold_in(key, 2)
    key_hot = jax.random.fold_in(key, 3)
    key_offset = jax.random.fold_in(key, 4)
    key_order = jax.random.fold_in(key, 5)
    counts = jax.random.randint(key_count, (DEVICES,), ROWS_DEV // 2, ROWS_DEV + 1)
    full_device = jax.random.randint(key_full, (), 0, DEVICES)
    counts = jnp.where(jnp.arange(DEVICES) == full_device, ROWS_DEV, counts).astype(jnp.int32)
    hottest = jax.random.randint(key_hot, (), 0, N_WIDE)
    offset = jax.random.randint(key_offset, (DEVICES, 1), 0, N_WIDE - 1)
    position = jnp.arange(ROWS_DEV, dtype=jnp.int32)[None, :]
    cyclic = (hottest + 1 + (offset + position) % (N_WIDE - 1)) % N_WIDE
    pattern = jnp.where(position < CAP, hottest, cyclic)
    noise = jax.random.randint(key_order, (DEVICES, ROWS_DEV), 0, 2 ** 16)
    score = jnp.where(position < counts[:, None], noise * ROWS_DEV + position, 2 ** 16 * ROWS_DEV + position)
    order = jnp.argsort(score, axis=1, stable=True)
    owner = jnp.take_along_axis(pattern, order, axis=1)
    return (counts, owner)


def passage_plan(key):
    counts, owner = route_plan(jax.random.fold_in(key, 7))
    within = jax.random.randint(jax.random.fold_in(key, 11), owner.shape, 0, LISTS_DEV)
    list_ids = (owner * LISTS_DEV + within).reshape(ROWS).astype(jnp.int32)
    codes = jax.random.randint(jax.random.fold_in(key, 13), (ROWS, M), 0, K).astype(jnp.int32)
    return (counts, list_ids, codes)


def clipped_normal(key, shape, scale, bound):
    return jnp.clip(scale * jax.random.normal(key, shape, jnp.float32), -bound, bound)


def centroid_field(key):
    sub = jax.random.fold_in(key, 17)
    return clipped_normal(sub, (LISTS, D), 1.0, 4.0)


def previous_words(key):
    sub = jax.random.fold_in(key, 19)
    return clipped_normal(sub, (M, K * DSUB), 1.0, 4.0)


def update_shift(key):
    sub = jax.random.fold_in(key, 23)
    return clipped_normal(sub, (M, K * DSUB), 0.5, 2.0)


def device_drift(key, index):
    sub = jax.random.fold_in(jax.random.fold_in(key, 31), index)
    ramp = index.astype(jnp.float32) / jnp.float32(DEVICES - 1)
    scale = 0.5 * jnp.exp(ramp * jnp.log(jnp.float32(6.0)))
    return scale * clipped_normal(sub, (D,), 1.0, 2.5)


def draw_rows(key, part):
    counts, list_ids, codes = passage_plan(key)
    centres = centroid_field(key).astype(jnp.bfloat16).astype(jnp.float32)
    moved = (previous_words(key) + update_shift(key)).reshape(M, K, DSUB)
    spaces = jnp.arange(M, dtype=jnp.int32)[None, :]
    noise_key = jax.random.fold_in(key, 29)

    def block(pieces):
        index, block_lists, block_codes = pieces
        sub = jax.random.fold_in(noise_key, index)
        noise = clipped_normal(sub, (ROWS_DEV, D), 0.3, 1.0)
        words = moved[spaces, block_codes].reshape(ROWS_DEV, D)
        drift = device_drift(key, index)[None, :]
        return (centres[block_lists] + words + noise + drift).astype(jnp.bfloat16)
    blocks = lax.map(block, (jnp.arange(DEVICES, dtype=jnp.int32), list_ids.reshape(DEVICES, ROWS_DEV), codes.reshape(DEVICES, ROWS_DEV, M)))
    return blocks.reshape(ROWS, D)


def draw_list_ids(key, part):
    counts, list_ids, codes = passage_plan(key)
    return list_ids


def draw_codes(key, part):
    counts, list_ids, codes = passage_plan(key)
    return codes


def draw_row_counts(key, part):
    counts, list_ids, codes = passage_plan(key)
    return counts.astype(jnp.int32)


def draw_centroids(key, part):
    return centroid_field(key).astype(jnp.bfloat16)


def draw_old_codebook(key, part):
    return previous_words(key)


def setup_inputs(seed: int = 0) -> dict:
    streams_of = jax.random.split(jax.random.key(seed), 7)
    rows = draw_rows(jax.random.fold_in(streams_of[6], 71), 0)
    list_ids = draw_list_ids(jax.random.fold_in(streams_of[6], 71), 0)
    codes = draw_codes(jax.random.fold_in(streams_of[6], 71), 0)
    row_counts = draw_row_counts(jax.random.fold_in(streams_of[6], 71), 0)
    centroids = draw_centroids(jax.random.fold_in(streams_of[6], 71), 0)
    old_codebook = draw_old_codebook(jax.random.fold_in(streams_of[6], 71), 0)
    return {"rows": rows, "list_ids": list_ids, "codes": codes, "row_counts": row_counts, "centroids": centroids, "old_codebook": old_codebook}


def reference(rows, list_ids, codes, row_counts, centroids, old_codebook):
    rows_b = rows.reshape(DEVICES, ROWS_DEV, D)
    lists_b = list_ids.reshape(DEVICES, ROWS_DEV)
    codes_b = codes.reshape(DEVICES, ROWS_DEV, M)
    position = jnp.arange(ROWS_DEV, dtype=jnp.int32)
    offsets = (jnp.arange(M, dtype=jnp.int32) * K)[None, :]

    def residual_of(block_rows, block_lists):
        return (block_rows.astype(jnp.float32) - centroids[block_lists].astype(jnp.float32)).astype(jnp.bfloat16)

    def absorb(carry, pieces):
        block_rows, block_lists, block_codes, count = pieces
        live_rows = (position < count).astype(jnp.float32)
        resid = residual_of(block_rows, block_lists).astype(jnp.float32) * live_rows[:, None]
        segment = (block_codes + offsets).reshape(ROWS_DEV * M)
        sums = carry[0] + jax.ops.segment_sum(resid.reshape(ROWS_DEV * M, DSUB), segment, num_segments=M * K)
        weights = jnp.broadcast_to(live_rows[:, None], (ROWS_DEV, M)).reshape(ROWS_DEV * M)
        counts = carry[1] + jax.ops.segment_sum(weights, segment, num_segments=M * K)
        return (sums, counts), None

    start = (jnp.zeros((M * K, DSUB), jnp.float32), jnp.zeros((M * K,), jnp.float32))
    (sums, counts), unused = lax.scan(absorb, start, (rows_b, lists_b, codes_b, row_counts))
    anchor = jnp.float32(ANCHOR)
    refit = (sums + anchor * old_codebook.reshape(M * K, DSUB)) / (counts[:, None] + anchor)
    table = refit.astype(jnp.bfloat16)

    def errors(pieces):
        block_rows, block_lists, block_codes, count = pieces
        resid = residual_of(block_rows, block_lists).astype(jnp.float32)
        segment = (block_codes + offsets).reshape(ROWS_DEV * M)
        decoded = table[segment].astype(jnp.float32).reshape(ROWS_DEV, D)
        diff = resid - decoded
        err = jnp.mean(diff * diff, axis=1)
        return jnp.where(position < count, err, jnp.float32(0.0))

    row_error = lax.map(errors, (rows_b, lists_b, codes_b, row_counts)).reshape(ROWS)
    return refit.reshape(M, K * DSUB), table.reshape(M, K * DSUB), row_error
```

```python
import functools

import jax
import jax.numpy as jnp
from jax import lax
from jax.experimental import pallas as pl
from jax.experimental.pallas import tpu as pltpu
from jax.sharding import PartitionSpec as P


K = 256
LOW = 4
HIGH = K // LOW
SUB = 16
LF = LOW * SUB
F32 = jnp.float32
BF16 = jnp.bfloat16
NT = (((1,), (1,)), ((), ()))


def iota(shape, dim, dtype=jnp.int32):
    return lax.broadcasted_iota(jnp.int32, shape, dim).astype(dtype)


def eye(n):
    return jnp.where(iota((n, n), 0) == iota((n, n), 1), 1.0, 0.0).astype(BF16)


def dot_nt(a, b):
    return lax.dot_general(a, b, NT, preferred_element_type=F32)


def whole(memory_space=pltpu.VMEM):
    return pl.BlockSpec(memory_space=memory_space)


def params():
    return pltpu.CompilerParams(vmem_limit_bytes=60 * 1024 * 1024)


def route_kernel(lists, count_ref, ids_ref, owner_ref, rank_ref, src_ref, lst_ref):
    n = ids_ref.shape[1]
    wide = src_ref.shape[0]
    lanes = src_ref.shape[1]
    blk = 256
    count = count_ref[0]
    tri = jnp.where(iota((blk, blk), 0) < iota((blk, blk), 1), 1.0, 0.0).astype(BF16)
    owners = iota((wide, blk), 0)
    ranks = iota((lanes, blk), 0, F32)
    acc = jnp.zeros((wide, 5 * lanes), F32)
    carry = jnp.zeros((wide, 1), F32)
    for j in range(n // blk):
        cols = slice(j * blk, (j + 1) * blk)
        ids = ids_ref[:, cols]
        pos = iota((1, blk), 1) + j * blk
        live = pos < count
        owner = ids // lists
        local = ids - owner * lists
        owner = jnp.where(live, owner, -1)
        member = jnp.where(owners == owner, 1.0, 0.0)
        member_b = member.astype(BF16)
        ahead = jnp.dot(member_b, tri, preferred_element_type=F32) + carry
        rank = jnp.sum(member * ahead, axis=0, keepdims=True)
        rank = jnp.where(live, rank, -1.0)
        carry = carry + jnp.sum(member, axis=1, keepdims=True)
        owner_ref[:, cols] = owner
        rank_ref[:, cols] = rank.astype(jnp.int32)
        hot = jnp.where(ranks == rank, 1.0, 0.0)
        stack = [hot]
        for value in (pos, local):
            high = value >> 6
            stack.append(hot * high.astype(F32))
            stack.append(hot * (value - (high << 6)).astype(F32))
        stack = jnp.concatenate(stack, axis=0).astype(BF16)
        acc = acc + dot_nt(member_b, stack)
    used = acc[:, :lanes] > 0.5
    src = acc[:, lanes : 2 * lanes] * 64.0 + acc[:, 2 * lanes : 3 * lanes]
    lst = acc[:, 3 * lanes : 4 * lanes] * 64.0 + acc[:, 4 * lanes :]
    src_ref[...] = jnp.where(used, src.astype(jnp.int32), n)
    lst_ref[...] = jnp.where(used, lst.astype(jnp.int32), 0)


def route(ids, count, wide, lists):
    n = ids.shape[0]
    return pl.pallas_call(
        functools.partial(route_kernel, lists),
        in_specs=[whole(pltpu.SMEM), whole()],
        out_specs=[whole()] * 4,
        out_shape=[
            jax.ShapeDtypeStruct((1, n), jnp.int32),
            jax.ShapeDtypeStruct((1, n), jnp.int32),
            jax.ShapeDtypeStruct((wide, 128), jnp.int32),
            jax.ShapeDtypeStruct((wide, 128), jnp.int32),
        ],
        compiler_params=params(),
        name="route",
    )(count, ids.reshape(1, n))


def pick_kernel(first, table_rows, index_ref, rows_ref, out_ref, tab, buf):
    per, cap, width = out_ref.shape
    groups = width // 128
    step = pl.program_id(0)

    @pl.when(step == 0)
    def _():
        def build(t, carry):
            r = pl.multiple_of(t * 16, 16)
            x = rows_ref[pl.ds(r, 16), :].astype(F32)
            for j in range(groups):
                tab[pl.ds(r * groups + j, 16, stride=groups), :] = x[:, j * 128 : (j + 1) * 128]
            return carry

        lax.fori_loop(0, table_rows // 16, build, 0)
        tab[table_rows * groups :, :] = jnp.zeros((groups, 128), F32)

    def fill(w, carry):
        for c in range(cap):
            i = index_ref[step * per + w, first + c]
            row = tab[pl.ds(pl.multiple_of(i * groups, groups), groups), :]
            buf[c * groups : (c + 1) * groups, :] = row
        for c in range(0, cap, 16):
            for j in range(groups):
                out_ref[w, c : c + 16, j * 128 : (j + 1) * 128] = buf[
                    pl.ds(c * groups + j, 16, stride=groups), :
                ].astype(BF16)
        return carry

    lax.fori_loop(0, per, fill, 0)


def pick(rows, index, first, cap):
    n, width = rows.shape
    wide = index.shape[0]
    per = 4
    groups = width // 128
    return pl.pallas_call(
        functools.partial(pick_kernel, first, n),
        grid_spec=pltpu.PrefetchScalarGridSpec(
            num_scalar_prefetch=1,
            grid=(wide // per,),
            in_specs=[whole()],
            out_specs=pl.BlockSpec((per, cap, width), lambda s, index: (s, 0, 0)),
            scratch_shapes=[
                pltpu.VMEM(((n + 1) * groups, 128), F32),
                pltpu.VMEM((cap * groups, 128), F32),
            ],
        ),
        out_shape=jax.ShapeDtypeStruct((wide, cap, width), BF16),
        compiler_params=params(),
        name="pick_rows",
    )(index, rows)


def codes_kernel(index_ref, count_ref, codes_ref, list_ref, out_ref, turned_ref, tab, buf):
    wide, _, lanes = out_ref.shape
    half = buf.shape[0] // 2
    n, spaces = codes_ref.shape
    codes = codes_ref[...].astype(F32).astype(BF16)
    one = eye(spaces)
    tab[0:n, :] = jnp.dot(codes, jnp.concatenate([one, one], axis=1), preferred_element_type=F32)
    tab[n:, :] = jnp.full((8, lanes), -1.0, F32)
    turned = dot_nt(one, codes)
    turned_ref[...] = jnp.where(iota((spaces, n), 1) < count_ref[0], turned, -1.0)
    left = iota((half, lanes), 1) < spaces

    def fill(w, carry):
        for c in range(2 * half):
            i = index_ref[w, c]
            buf[c : c + 1, :] = tab[pl.ds(i, 1), :]
        out_ref[w, 0:half, :] = jnp.where(left, buf[0:half, :], buf[half:, :]).astype(BF16)
        listed = jnp.broadcast_to(list_ref[pl.ds(w, 1), :], (16, lanes))
        listed = jnp.where(iota((16, lanes), 0) == 0, listed >> 6, listed & 63)
        out_ref[w, half:, :] = listed.astype(F32).astype(BF16)
        return carry

    lax.fori_loop(0, wide, fill, 0)


def pick_codes(codes, index, lists, count, cap):
    n, spaces = codes.shape
    wide = index.shape[0]
    return pl.pallas_call(
        codes_kernel,
        in_specs=[whole(pltpu.SMEM), whole(pltpu.SMEM), whole(), whole()],
        out_specs=[whole(), whole()],
        out_shape=[
            jax.ShapeDtypeStruct((wide, cap // 2 + 16, 2 * spaces), BF16),
            jax.ShapeDtypeStruct((spaces, n), F32),
        ],
        scratch_shapes=[pltpu.VMEM((n + 8, 2 * spaces), F32), pltpu.VMEM((cap, 2 * spaces), F32)],
        compiler_params=params(),
        name="pick_codes",
    )(index, count, codes, lists)


def turn_kernel(x_ref, out_ref, list_ref):
    wide, rows, lanes = x_ref.shape
    half = rows - 16
    out_ref[...] = dot_nt(eye(lanes), x_ref[:, 0:half, :].reshape(-1, lanes))

    def unpack(w, carry):
        listed = x_ref[w, half:, :].astype(F32)
        list_ref[pl.ds(w, 1), :] = (listed[0:1] * 64.0 + listed[1:2]).astype(jnp.int32)
        return carry

    lax.fori_loop(0, wide, unpack, 0)


def turn(x):
    wide, rows, lanes = x.shape
    return pl.pallas_call(
        turn_kernel,
        in_specs=[whole()],
        out_specs=[whole(), whole()],
        out_shape=[
            jax.ShapeDtypeStruct((lanes, wide * (rows - 16)), F32),
            jax.ShapeDtypeStruct((wide, lanes), jnp.int32),
        ],
        compiler_params=params(),
        name="turn_codes",
    )(x)


def split_code(row):
    high = jnp.floor(row * (1.0 / LOW))
    return high, row - LOW * high


def spread(row, rows=SUB):
    return jnp.broadcast_to(row, (rows, row.shape[1]))


def high_at(q):
    return 2 * (q % (HIGH // 2)) + q // (HIGH // 2)


def high_hot(high, t, zero, one):
    want = high_at(iota((16, high.shape[1]), 0) + t * 16).astype(F32).astype(BF16)
    return jnp.where(high == want, one, zero)


def gram_kernel(sign, counted, chunk, *refs):
    if counted:
        x_ref, codes_ref, out_ref, turned, hot, val, acc = refs
        prev_ref = None
    else:
        x_ref, codes_ref, prev_ref, out_ref, turned, hot, val, acc = refs
    lanes = x_ref.shape[-1]
    x = x_ref[...].reshape(-1, lanes)
    n = x.shape[0]
    spaces = lanes // SUB
    turned[...] = dot_nt(eye(lanes), x).astype(BF16)
    step = pl.program_id(1)
    for g in range(spaces // 4):
        acc[...] = jnp.zeros_like(acc)

        def absorb(t, carry):
            cols = pl.ds(pl.multiple_of(t * chunk, chunk), chunk)
            zero = jnp.zeros((16, chunk), BF16)
            one = jnp.ones((16, chunk), BF16)
            codes = codes_ref[:, cols]
            if counted:
                rows = iota((16, chunk), 0)
                lows = jnp.full((16, chunk), -2.0, F32)
            for i in range(4):
                m = g * 4 + i
                high, low = split_code(codes[m : m + 1, :])
                low_f = spread(low)
                high, low = spread(high).astype(BF16), low_f.astype(BF16)
                for q in range(HIGH // 16):
                    hot[i * HIGH + q * 16 : i * HIGH + (q + 1) * 16, :] = high_hot(high, q, zero, one)
                piece = turned[m * SUB : (m + 1) * SUB, cols]
                for k in range(LOW):
                    val[i * LF + k * SUB : i * LF + (k + 1) * SUB, :] = jnp.where(
                        low == jnp.full((16, chunk), k, BF16), piece, zero
                    )
                if counted:
                    lows = jnp.where(rows // LOW == i, low_f, lows)
            if counted:
                val[4 * LF :, :] = jnp.where((rows % LOW).astype(F32) == lows, 1.0, 0.0).astype(BF16)
            acc[...] += dot_nt(val[...], hot[...])
            return carry

        lax.fori_loop(0, n // chunk, absorb, 0)
        for i in range(4):
            m = g * 4 + i
            cols = slice(i * HIGH, (i + 1) * HIGH)
            top = acc[i * LF : i * LF + LF // 2, cols]
            low = acc[i * LF + LF // 2 : (i + 1) * LF, cols]
            sums = sign * jnp.concatenate([top, low], axis=1)
            if counted:
                out_ref[m, 0 : LF // 2, :] = sums
                base = 4 * LF + i * LOW
                cnt = jnp.concatenate([acc[base : base + 2, cols], acc[base + 2 : base + 4, cols]], axis=1)
                out_ref[m, LF // 2 : LF // 2 + 8, :] = jnp.concatenate([cnt, jnp.zeros((6, 2 * HIGH), F32)], axis=0)
            else:

                @pl.when(step == 0)
                def _():
                    out_ref[m, 0 : LF // 2, :] = prev_ref[m, 0 : LF // 2, :] + sums
                    out_ref[m, LF // 2 : LF // 2 + 8, :] = prev_ref[m, LF // 2 : LF // 2 + 8, :]

                @pl.when(step > 0)
                def _():
                    out_ref[m, 0 : LF // 2, :] += sums


def gram(x, codes, prev=None):
    groups, halves, cap, width = x.shape
    spaces = width // SUB
    n = groups * cap
    counted = prev is None
    chunk = 512
    assert n % chunk == 0
    state = pl.BlockSpec((8, LF // 2 + 8, 128), lambda f, h: (f, 0, 0))
    in_specs = [
        pl.BlockSpec((groups, 1, cap, 128), lambda f, h: (0, h, 0, f)),
        pl.BlockSpec((8, n), lambda f, h: (h * (spaces // 8) + f, 0)),
    ]
    rows = 4 * LF + (16 if counted else 0)
    return pl.pallas_call(
        functools.partial(gram_kernel, 1.0 if counted else -1.0, counted, chunk),
        grid=(spaces // 8, halves),
        in_specs=in_specs + ([] if counted else [state]),
        out_specs=state,
        out_shape=jax.ShapeDtypeStruct((spaces, LF // 2 + 8, 128), F32),
        scratch_shapes=[
            pltpu.VMEM((128, n), BF16),
            pltpu.VMEM((4 * HIGH, chunk), BF16),
            pltpu.VMEM((rows, chunk), BF16),
            pltpu.VMEM((rows, 4 * HIGH), F32),
        ],
        compiler_params=params(),
        name="row_sums" if counted else "centroid_sums",
    )(x, codes, *([] if counted else [prev]))


def refit_kernel(anchor, total_ref, old_ref, out_ref):
    total = total_ref[...]
    half = LF // 2
    sums = jnp.concatenate([total[0:half, 0:HIGH], total[0:half, HIGH:]], axis=0)
    counts = [total[half + k % 2 : half + k % 2 + 1, (k // 2) * HIGH : (k // 2 + 1) * HIGH] for k in range(LOW)]
    counts = jnp.concatenate([spread(c) for c in counts], axis=0)
    both = jnp.concatenate([sums, counts], axis=1)
    both = jnp.concatenate([both, jnp.zeros_like(both)], axis=0)
    both = both.T
    h = HIGH // 2
    sums = jnp.concatenate([both[0:h, 0:LF], both[h : 2 * h, 0:LF]], axis=1)
    counts = jnp.concatenate([both[2 * h : 3 * h, 0:LF], both[3 * h : 4 * h, 0:LF]], axis=1)
    out_ref[...] = (sums + anchor * old_ref[...]) / (counts + anchor)


def refit(total, old, anchor):
    return pl.pallas_call(
        functools.partial(refit_kernel, anchor),
        in_specs=[whole()] * 2,
        out_specs=whole(),
        out_shape=jax.ShapeDtypeStruct(old.shape, F32),
        compiler_params=params(),
        name="refit",
    )(total, old)


def error_kernel(rows_ref, cent_ref, codes_ref, table_ref, out_ref, blocks, resid):
    width = resid.shape[1]
    n = resid.shape[0]
    spaces = width // SUB

    @pl.when(pl.program_id(0) == 0)
    def _():
        blocks[...] = jnp.zeros_like(blocks)
        one = eye(LF)

        def build(g, carry):
            for i in range(4):
                tab = table_ref[g * 4 + i].astype(BF16)
                tab = jnp.concatenate([tab[:, 0:LF], tab[:, LF:]], axis=0)
                blocks[g, i * LF : (i + 1) * LF, i * HIGH : (i + 1) * HIGH] = dot_nt(one, tab).astype(BF16)
            return carry

        lax.fori_loop(0, spaces // 4, build, 0)

    rows = rows_ref[...].reshape(n, width).astype(F32)
    cent = cent_ref[...].reshape(n, width).astype(F32)
    resid[...] = (rows - cent).astype(BF16)
    one = eye(128)
    zero16 = jnp.zeros((16, n), BF16)
    one16 = jnp.ones((16, n), BF16)

    def part(f, acc):
        turned = dot_nt(one, resid[:, pl.ds(pl.multiple_of(f * 128, 128), 128)])
        codes = codes_ref[pl.ds(pl.multiple_of(f * 8, 8), 8), :]
        for g in range(2):
            hot, lows = [], []
            for i in range(4):
                m = g * 4 + i
                high, low = split_code(codes[m : m + 1, :])
                lows.append(low)
                high = spread(high).astype(BF16)
                for q in range(HIGH // 16):
                    hot.append(high_hot(high, q, zero16, one16))
            hot = jnp.concatenate(hot, axis=0)
            words = jnp.dot(blocks[f * 2 + g], hot, preferred_element_type=F32)
            for i in range(4):
                m = g * 4 + i
                low = spread(lows[i])
                word = words[i * LF + (LOW - 1) * SUB : (i + 1) * LF, :]
                for k in range(LOW - 1):
                    word = jnp.where(low == float(k), words[i * LF + k * SUB : i * LF + (k + 1) * SUB, :], word)
                diff = turned[m * SUB : (m + 1) * SUB, :] - word
                acc = acc + diff * diff
        return acc

    acc = lax.fori_loop(0, width // 128, part, jnp.zeros((SUB, n), F32))
    out_ref[...] = jnp.sum(acc, axis=0, keepdims=True) * (1.0 / width)


def errors(rows, cent, codes, table, half):
    wide, cap, width = rows.shape
    spaces = width // SUB
    per = 8
    n = per * cap
    return pl.pallas_call(
        error_kernel,
        grid=(wide // per,),
        in_specs=[
            pl.BlockSpec((per, cap, width), lambda s: (s, 0, 0)),
            pl.BlockSpec((per, 1, cap, width), lambda s: (s, half, 0, 0)),
            pl.BlockSpec((spaces, n), lambda s: (half, s)),
            whole(),
        ],
        out_specs=pl.BlockSpec((1, n), lambda s: (0, s)),
        out_shape=jax.ShapeDtypeStruct((1, wide * cap), F32),
        scratch_shapes=[
            pltpu.VMEM((spaces // 4, 4 * LF, 4 * HIGH), BF16),
            pltpu.VMEM((n, width), BF16),
        ],
        compiler_params=params(),
        name="errors",
    )(rows, cent, codes, table)


def home_kernel(owner_ref, rank_ref, first_ref, second_ref, out_ref):
    wide, cap = first_ref.shape
    n = owner_ref.shape[1]
    owner = owner_ref[...]
    rank = rank_ref[...]
    member = jnp.where(iota((wide, n), 0) == owner, 1.0, 0.0).astype(BF16)
    member = jnp.concatenate([member] * 3, axis=0)
    one = eye(cap)
    total = jnp.zeros((1, n), F32)
    for h, ref in enumerate((first_ref, second_ref)):
        left = ref[...]
        pieces = []
        for _ in range(3):
            piece = left.astype(BF16)
            left = left - piece.astype(F32)
            pieces.append(dot_nt(one, piece))
        pieces = jnp.concatenate(pieces, axis=1).astype(BF16)
        slots = jnp.dot(pieces, member, preferred_element_type=F32)
        mine = iota((cap, n), 0) + h * cap == rank
        total = total + jnp.sum(jnp.where(mine, slots, 0.0), axis=0, keepdims=True)
    out_ref[...] = total


def bring_home(owner, rank, first, second):
    n = owner.shape[1]
    return pl.pallas_call(
        home_kernel,
        in_specs=[whole()] * 4,
        out_specs=whole(),
        out_shape=jax.ShapeDtypeStruct((1, n), F32),
        compiler_params=params(),
        name="bring_home",
    )(owner, rank, first, second)


def exchange(x):
    return lax.all_to_all(x, "wide", split_axis=0, concat_axis=0, tiled=True)


def swap(x, bit):
    if bit is None:
        return lax.ppermute(x, "narrow", [(0, 1), (1, 0)])
    return lax.ppermute(x, "wide", [(i, i ^ (1 << bit)) for i in range(lax.axis_size("wide"))])


def share_bits():
    last = lax.axis_size("wide").bit_length() - 2
    order = sorted(range(last + 1), key=lambda b: (b % 2, -b))
    return [None] + order[:-1], order[-1]


def own_bit(bit):
    return lax.axis_index("narrow") if bit is None else (lax.axis_index("wide") >> bit) & 1


def reduce_shares(x):
    bits, rest = share_bits()
    for bit in bits:
        x = x.reshape((2, x.shape[0] // 2) + x.shape[1:])
        here = own_bit(bit)
        away = lax.dynamic_index_in_dim(x, 1 - here, 0, keepdims=False)
        x = lax.dynamic_index_in_dim(x, here, 0, keepdims=False) + swap(away, bit)
    return x + swap(x, rest)


def gather_shares(x):
    bits, _ = share_bits()
    for bit in reversed(bits):
        other = swap(x, bit)
        x = jnp.where(own_bit(bit) == 0, jnp.stack([x, other]), jnp.stack([other, x]))
        x = x.reshape((-1,) + x.shape[2:])
    return x


def own_share():
    share = jnp.int32(0)
    for bit in share_bits()[0]:
        share = share * 2 + own_bit(bit)
    return share


def refit_step(rows, list_ids, codes, row_counts, centroids, old_codebook):
    local_rows, width = rows.shape
    spaces = codes.shape[1]
    wide = lax.axis_size("wide")
    cap = 2 * local_rows // wide
    half = cap // 2
    lists = centroids.shape[0]
    own = lax.axis_index("wide")
    anchor = float(local_rows * lax.axis_size("narrow") * wide // (4 * K))

    owner, rank, src, lst = route(list_ids, row_counts, wide, lists)
    sent_codes, codes_local = pick_codes(codes, src, lst, row_counts, cap)
    got_codes = exchange(sent_codes)
    got_first = exchange(pick(rows, src, 0, half))
    got_second = exchange(pick(rows, src, half, half))

    sums = gram(rows.reshape(1, 1, local_rows, width), codes_local)
    codes_slots, got_lists = turn(got_codes)
    cent = pick(centroids, got_lists, 0, cap).reshape(wide, 2, half, width)
    sums = gram(cent, codes_slots, sums)
    mine = reduce_shares(sums)
    old = lax.dynamic_slice_in_dim(old_codebook, own_share(), 1, 0).reshape(K * SUB // 128, 128)
    word = refit(mine[0], old, anchor)
    book = gather_shares(word[None])
    codebook = book.reshape(spaces, K * SUB)
    search_table = lax.dynamic_slice_in_dim(codebook, own, 1, 0).astype(BF16)

    err_first = errors(got_first, cent, codes_slots, book, 0)
    err_second = errors(got_second, cent, codes_slots, book, 1)
    back_first = exchange(err_first.reshape(wide, half))
    back_second = exchange(err_second.reshape(wide, half))
    row_error = bring_home(owner, rank, back_first, back_second).reshape(local_rows)
    return (codebook, search_table, row_error)


def solution(mesh):
    in_specs = (
        P(("narrow", "wide"), None),
        P(("narrow", "wide")),
        P(("narrow", "wide"), None),
        P(("narrow", "wide")),
        P("wide", None),
        P(),
    )
    out_specs = (P(), P("wide", None), P(("narrow", "wide")))
    return jax.shard_map(refit_step, mesh=mesh, in_specs=in_specs, out_specs=out_specs, check_vma=False)
```

```python
import functools

import jax
import jax.numpy as jnp
from jax import lax
from jax.experimental import pallas as pl
from jax.experimental.pallas import tpu as pltpu
from jax.sharding import PartitionSpec as P


K = 256
LOW = 4
HIGH = K // LOW
SUB = 16
LF = LOW * SUB
UNROLL = 4
F32 = jnp.float32
BF16 = jnp.bfloat16
NT = (((1,), (1,)), ((), ()))


def iota(shape, dim, dtype=jnp.int32):
    return lax.broadcasted_iota(jnp.int32, shape, dim).astype(dtype)


def eye(n):
    return jnp.where(iota((n, n), 0) == iota((n, n), 1), 1.0, 0.0).astype(BF16)


def dot_nt(a, b):
    return lax.dot_general(a, b, NT, preferred_element_type=F32)


def whole(memory_space=pltpu.VMEM):
    return pl.BlockSpec(memory_space=memory_space)


def params():
    return pltpu.CompilerParams(vmem_limit_bytes=60 * 1024 * 1024)


def route_kernel(lists, count_ref, ids_ref, owner_ref, rank_ref, src_ref, scaled_ref, lst_ref):
    n = ids_ref.shape[1]
    wide = src_ref.shape[0]
    lanes = src_ref.shape[1]
    blk = 256
    count = count_ref[0]
    tri = jnp.where(iota((blk, blk), 0) < iota((blk, blk), 1), 1.0, 0.0).astype(BF16)
    owners = iota((wide, blk), 0)
    ranks = iota((lanes, blk), 0, F32)
    acc = jnp.zeros((wide, 5 * lanes), F32)
    carry = jnp.zeros((wide, 1), F32)
    for j in range(n // blk):
        cols = slice(j * blk, (j + 1) * blk)
        ids = ids_ref[:, cols]
        pos = iota((1, blk), 1) + j * blk
        live = pos < count
        owner = ids // lists
        local = ids - owner * lists
        owner = jnp.where(live, owner, -1)
        member = jnp.where(owners == owner, 1.0, 0.0)
        member_b = member.astype(BF16)
        ahead = jnp.dot(member_b, tri, preferred_element_type=F32) + carry
        rank = jnp.sum(member * ahead, axis=0, keepdims=True)
        rank = jnp.where(live, rank, -1.0)
        carry = carry + jnp.sum(member, axis=1, keepdims=True)
        owner_ref[:, cols] = owner
        rank_ref[:, cols] = rank.astype(jnp.int32)
        hot = jnp.where(ranks == rank, 1.0, 0.0)
        stack = [hot]
        for value in (pos, local):
            high = value >> 6
            stack.append(hot * high.astype(F32))
            stack.append(hot * (value - (high << 6)).astype(F32))
        stack = jnp.concatenate(stack, axis=0).astype(BF16)
        acc = acc + dot_nt(member_b, stack)
    used = acc[:, :lanes] > 0.5
    src = acc[:, lanes : 2 * lanes] * 64.0 + acc[:, 2 * lanes : 3 * lanes]
    lst = acc[:, 3 * lanes : 4 * lanes] * 64.0 + acc[:, 4 * lanes :]
    src = jnp.where(used, src.astype(jnp.int32), n)
    src_ref[...] = src
    scaled_ref[...] = src * 8
    lst_ref[...] = jnp.where(used, lst.astype(jnp.int32), 0)


def route(ids, count, wide, lists):
    n = ids.shape[0]
    return pl.pallas_call(
        functools.partial(route_kernel, lists),
        in_specs=[whole(pltpu.SMEM), whole()],
        out_specs=[whole()] * 5,
        out_shape=[
            jax.ShapeDtypeStruct((1, n), jnp.int32),
            jax.ShapeDtypeStruct((1, n), jnp.int32),
            jax.ShapeDtypeStruct((wide, 128), jnp.int32),
            jax.ShapeDtypeStruct((wide, 128), jnp.int32),
            jax.ShapeDtypeStruct((wide, 128), jnp.int32),
        ],
        compiler_params=params(),
        name="route",
    )(count, ids.reshape(1, n))


def pick_kernel(first, table_rows, index_ref, rows_ref, out_ref, tab, *bufs):
    per, cap, width = out_ref.shape
    groups = width // 128
    step = pl.program_id(0)

    @pl.when(step == 0)
    def _():
        def build(t, carry):
            r = pl.multiple_of(t * 16, 16)
            x = rows_ref[pl.ds(r, 16), :].astype(F32)
            for j in range(groups):
                tab[pl.ds(r * groups + j, 16, stride=groups), :] = x[:, j * 128 : (j + 1) * 128]
            return carry

        lax.fori_loop(0, table_rows // 16, build, 0)
        tab[table_rows * groups :, :] = jnp.zeros((groups, 128), F32)

    def fill(t, carry):
        for k, buf in enumerate(bufs):
            w = t * len(bufs) + k
            for c in range(cap):
                i = index_ref[step * per + w, first + c]
                row = tab[pl.ds(pl.multiple_of(i, groups), groups), :]
                buf[c * groups : (c + 1) * groups, :] = row
        for k, buf in enumerate(bufs):
            w = t * len(bufs) + k
            for c in range(0, cap, 16):
                for j in range(groups):
                    out_ref[w, c : c + 16, j * 128 : (j + 1) * 128] = buf[
                        pl.ds(c * groups + j, 16, stride=groups), :
                    ].astype(BF16)
        return carry

    lax.fori_loop(0, per // len(bufs), fill, 0)


def pick(rows, index, first, cap):
    n, width = rows.shape
    wide = index.shape[0]
    per = 4
    groups = width // 128
    return pl.pallas_call(
        functools.partial(pick_kernel, first, n),
        grid_spec=pltpu.PrefetchScalarGridSpec(
            num_scalar_prefetch=1,
            grid=(wide // per,),
            in_specs=[whole()],
            out_specs=pl.BlockSpec((per, cap, width), lambda s, index: (s, 0, 0)),
            scratch_shapes=[
                pltpu.VMEM(((n + 1) * groups, 128), F32),
                pltpu.VMEM((cap * groups, 128), F32),
                pltpu.VMEM((cap * groups, 128), F32),
            ],
        ),
        out_shape=jax.ShapeDtypeStruct((wide, cap, width), BF16),
        compiler_params=params(),
        name="pick_rows",
    )(index, rows)


def codes_kernel(index_ref, count_ref, codes_ref, list_ref, out_ref, turned_ref, tab, buf):
    wide, _, lanes = out_ref.shape
    cap = buf.shape[0]
    half = cap // 2
    spaces, n = codes_ref.shape
    codes = codes_ref[...].astype(F32)
    one = eye(spaces)
    both = jnp.concatenate([one, one], axis=1)
    tab[0:n, :] = lax.dot_general(codes.astype(BF16), both, (((0,), (0,)), ((), ())), preferred_element_type=F32)
    tab[n:, :] = jnp.full((8, lanes), -1.0, F32)
    turned_ref[...] = jnp.where(iota((spaces, n), 1) < count_ref[0], codes, -1.0)
    left = iota((16, lanes), 1) < spaces

    def fill(w, carry):
        for c in range(cap):
            i = index_ref[w, c]
            buf[c : c + 1, :] = tab[pl.ds(i, 1), :]
        for c in range(0, cap, 32):
            pair = jnp.where(left, buf[c : c + 16, :], buf[c + 16 : c + 32, :])
            out_ref[w, c // 2 : c // 2 + 16, :] = pair.astype(BF16)
        listed = jnp.broadcast_to(list_ref[pl.ds(w, 1), :], (8, lanes))
        listed = jnp.where(iota((8, lanes), 0) == 0, listed >> 6, listed & 63)
        out_ref[w, half:, :] = listed.astype(F32).astype(BF16)
        return carry

    lax.fori_loop(0, wide, fill, 0)


def pick_codes(codes, index, lists, count, cap):
    codes = codes.T
    spaces, n = codes.shape
    wide = index.shape[0]
    return pl.pallas_call(
        codes_kernel,
        in_specs=[whole(pltpu.SMEM), whole(pltpu.SMEM), whole(), whole()],
        out_specs=[whole(), whole()],
        out_shape=[
            jax.ShapeDtypeStruct((wide, cap // 2 + 8, 2 * spaces), BF16),
            jax.ShapeDtypeStruct((spaces, n), F32),
        ],
        scratch_shapes=[pltpu.VMEM((n + 8, 2 * spaces), F32), pltpu.VMEM((cap, 2 * spaces), F32)],
        compiler_params=params(),
        name="pick_codes",
    )(index, count, codes, lists)


def turn_kernel(x_ref, out_ref):
    wide, rows, lanes = x_ref.shape
    spaces = lanes // 2
    n = wide * 16
    one = eye(lanes)
    for u in range((rows - 8) // 16):
        pair = dot_nt(one, x_ref[:, u * 16 : (u + 1) * 16, :].reshape(n, lanes))
        out_ref[:, 2 * u * n : (2 * u + 1) * n] = pair[0:spaces, :]
        out_ref[:, (2 * u + 1) * n : (2 * u + 2) * n] = pair[spaces:, :]


def turn(x):
    wide, rows, lanes = x.shape
    return pl.pallas_call(
        turn_kernel,
        in_specs=[whole()],
        out_specs=whole(),
        out_shape=jax.ShapeDtypeStruct((lanes // 2, 2 * wide * (rows - 8)), F32),
        compiler_params=params(),
        name="turn_codes",
    )(x)


def lists_kernel(scale, x_ref, out_ref):
    for w in range(x_ref.shape[0]):
        listed = x_ref[w].astype(F32)
        out_ref[w : w + 1, :] = ((listed[0:1] * 64.0 + listed[1:2]) * scale).astype(jnp.int32)


def lists_of(x, scale):
    wide, rows, lanes = x.shape
    return pl.pallas_call(
        functools.partial(lists_kernel, scale),
        grid=(1,),
        in_specs=[pl.BlockSpec((wide, 8, lanes), lambda i: (0, rows // 8 - 1, 0))],
        out_specs=pl.BlockSpec((wide, lanes), lambda i: (0, 0)),
        out_shape=jax.ShapeDtypeStruct((wide, lanes), jnp.int32),
        compiler_params=params(),
        name="lists",
    )(x)


def split_code(row):
    high = jnp.floor(row * (1.0 / LOW))
    return high, row - LOW * high


def spread(row, rows=SUB):
    return jnp.broadcast_to(row, (rows, row.shape[1]))


def high_at(q):
    return 2 * (q % (HIGH // 2)) + q // (HIGH // 2)


def gram_kernel(sign, counted, chunk, *refs):
    if counted:
        x_ref, codes_ref, out_ref, acc = refs
        prev_ref = None
    else:
        x_ref, codes_ref, prev_ref, out_ref, acc = refs
    groups, _, rows, lanes = x_ref.shape
    spaces = lanes // SUB
    per = chunk // rows
    n = codes_ref.shape[1]
    zero = jnp.zeros((16, chunk), BF16)
    one = jnp.ones((16, chunk), BF16)
    want = [high_at(iota((16, chunk), 0) + q * 16).astype(F32).astype(BF16) for q in range(HIGH // 16)]
    place = iota((16, chunk), 0)
    acc[...] = jnp.zeros_like(acc)

    def absorb(t, carry):
        v = t // (groups // per)
        first = pl.multiple_of(t % (groups // per) * per, per)
        x = x_ref[pl.ds(first, per), v].reshape(chunk, lanes)
        turned = x.T
        high8, low8 = split_code(codes_ref[:, pl.ds(pl.multiple_of(t * chunk, chunk), chunk)])
        for g in range(spaces // 4):
            hot, val = [], []
            lows = jnp.full((16, chunk), -2.0, F32)
            for i in range(4):
                m = g * 4 + i
                high = spread(high8[m : m + 1, :]).astype(BF16)
                low_f = spread(low8[m : m + 1, :])
                low = low_f.astype(BF16)
                hot += [jnp.where(high == w, one, zero) for w in want]
                piece = turned[m * SUB : (m + 1) * SUB, :]
                val += [jnp.where(low == jnp.full((16, chunk), k, BF16), piece, zero) for k in range(LOW)]
                if counted:
                    lows = jnp.where(place // LOW == i, low_f, lows)
            if counted:
                val.append(jnp.where((place % LOW).astype(F32) == lows, 1.0, 0.0).astype(BF16))
            acc[g] += dot_nt(jnp.concatenate(val, axis=0), jnp.concatenate(hot, axis=0))
        return carry

    lax.fori_loop(0, n // chunk, absorb, 0, unroll=2)
    for m in range(spaces):
        g, i = m // 4, m % 4
        cols = slice(i * HIGH, (i + 1) * HIGH)
        top = acc[g, i * LF : i * LF + LF // 2, cols]
        low = acc[g, i * LF + LF // 2 : (i + 1) * LF, cols]
        sums = sign * jnp.concatenate([top, low], axis=1)
        if counted:
            out_ref[m, 0 : LF // 2, :] = sums
            base = 4 * LF + i * LOW
            cnt = jnp.concatenate([acc[g, base : base + 2, cols], acc[g, base + 2 : base + 4, cols]], axis=1)
            out_ref[m, LF // 2 :, :] = jnp.concatenate([cnt, jnp.zeros((6, 2 * HIGH), F32)], axis=0)
        else:
            out_ref[m, 0 : LF // 2, :] = prev_ref[m, 0 : LF // 2, :] + sums
            out_ref[m, LF // 2 :, :] = prev_ref[m, LF // 2 :, :]


def gram(x, codes, block=0, prev=None):
    groups, pieces, rows, width = x.shape
    spaces = width // SUB
    n = groups * pieces * rows
    counted = prev is None
    chunk = 512
    assert n % chunk == 0 and chunk % rows == 0
    state = pl.BlockSpec((8, LF // 2 + 8, 128), lambda f: (f, 0, 0))
    in_specs = [
        pl.BlockSpec((groups, pieces, rows, 128), lambda f: (0, 0, 0, f)),
        pl.BlockSpec((8, n), lambda f: (f, block)),
    ]
    high = 4 * LF + (16 if counted else 0)
    return pl.pallas_call(
        functools.partial(gram_kernel, 1.0 if counted else -1.0, counted, chunk),
        grid=(spaces // 8,),
        in_specs=in_specs + ([] if counted else [state]),
        out_specs=state,
        out_shape=jax.ShapeDtypeStruct((spaces, LF // 2 + 8, 128), F32),
        scratch_shapes=[
            pltpu.VMEM((2, high, 4 * HIGH), F32),
        ],
        compiler_params=params(),
        name="row_sums" if counted else "centroid_sums",
    )(x, codes, *([] if counted else [prev]))


def refit_kernel(anchor, total_ref, old_ref, out_ref):
    half = LF // 2
    h = HIGH // 2
    for m in range(out_ref.shape[0]):
        total = total_ref[m]
        sums = jnp.concatenate([total[0:half, 0:HIGH], total[0:half, HIGH:]], axis=0)
        counts = [total[half + k % 2 : half + k % 2 + 1, (k // 2) * HIGH : (k // 2 + 1) * HIGH] for k in range(LOW)]
        counts = jnp.concatenate([spread(c) for c in counts], axis=0)
        both = jnp.concatenate([sums, counts], axis=1)
        both = jnp.concatenate([both, jnp.zeros_like(both)], axis=0)
        both = both.T
        sums = jnp.concatenate([both[0:h, 0:LF], both[h : 2 * h, 0:LF]], axis=1)
        counts = jnp.concatenate([both[2 * h : 3 * h, 0:LF], both[3 * h : 4 * h, 0:LF]], axis=1)
        out_ref[m] = (sums + anchor * old_ref[m]) / (counts + anchor)


def refit(total, old, anchor):
    return pl.pallas_call(
        functools.partial(refit_kernel, anchor),
        in_specs=[whole()] * 2,
        out_specs=whole(),
        out_shape=jax.ShapeDtypeStruct(old.shape, F32),
        compiler_params=params(),
        name="refit",
    )(total, old)


def tiles_kernel(table_ref, out_ref):
    out_ref[...] = jnp.zeros_like(out_ref)
    one = eye(LF)

    def build(g, carry):
        for i in range(4):
            tab = table_ref[g * 4 + i].astype(BF16)
            tab = jnp.concatenate([tab[:, 0:LF], tab[:, LF:]], axis=0)
            out_ref[g, i * LF : (i + 1) * LF, i * HIGH : (i + 1) * HIGH] = dot_nt(one, tab).astype(BF16)
        return carry

    lax.fori_loop(0, out_ref.shape[0], build, 0)


def tiles(table):
    return pl.pallas_call(
        tiles_kernel,
        in_specs=[whole()],
        out_specs=whole(),
        out_shape=jax.ShapeDtypeStruct((table.shape[0] // 4, 4 * LF, 4 * HIGH), BF16),
        compiler_params=params(),
        name="decode_tiles",
    )(table)


def error_kernel(rows_ref, cent_ref, codes_ref, blocks, out_ref, resid):
    width = resid.shape[1]
    n = resid.shape[0]
    resid[...] = rows_ref[...].reshape(n, width) - cent_ref[...].reshape(n, width)
    cols = 512
    zero16 = jnp.zeros((16, cols), BF16)
    one16 = jnp.ones((16, cols), BF16)
    want = [high_at(iota((16, cols), 0) + q * 16).astype(F32).astype(BF16) for q in range(HIGH // 16)]

    def group(t, carry):
        here = pl.ds(pl.multiple_of(t * cols, cols), cols)

        def part(f, acc):
            turned = resid[here, pl.ds(pl.multiple_of(f * 128, 128), 128)].T.astype(F32)
            high8, low8 = split_code(codes_ref[pl.ds(pl.multiple_of(f * 8, 8), 8), here])
            for g in range(2):
                hot = []
                for i in range(4):
                    high = spread(high8[g * 4 + i : g * 4 + i + 1, :]).astype(BF16)
                    hot += [jnp.where(high == w, one16, zero16) for w in want]
                words = jnp.dot(blocks[f * 2 + g], jnp.concatenate(hot, axis=0), preferred_element_type=F32)
                for i in range(4):
                    m = g * 4 + i
                    low = spread(low8[m : m + 1, :], 8)
                    masks = [low == float(k) for k in range(LOW - 1)]
                    for s in range(0, SUB, 8):
                        word = words[i * LF + (LOW - 1) * SUB + s : i * LF + (LOW - 1) * SUB + s + 8, :]
                        for k in range(LOW - 1):
                            word = jnp.where(masks[k], words[i * LF + k * SUB + s : i * LF + k * SUB + s + 8, :], word)
                        diff = turned[m * SUB + s : m * SUB + s + 8, :] - word
                        acc = acc + diff * diff
            return acc

        acc = lax.fori_loop(0, width // 128, part, jnp.zeros((8, cols), F32), unroll=UNROLL)
        err = jnp.sum(acc, axis=0, keepdims=True) * (1.0 / width)
        for i in range(cols // 128):
            out_ref[pl.ds(t * (cols // 128) + i, 1), :] = err[:, i * 128 : (i + 1) * 128]
        return carry

    lax.fori_loop(0, n // cols, group, 0)


def errors(rows, cent, codes, blocks, first):
    wide, pieces, _, width = cent.shape
    spaces = width // SUB
    n = wide * 16
    return pl.pallas_call(
        error_kernel,
        grid=(pieces,),
        in_specs=[
            pl.BlockSpec((wide, 1, 16, width), lambda v: (0, first + v, 0, 0)),
            pl.BlockSpec((wide, 1, 16, width), lambda v: (0, v, 0, 0)),
            pl.BlockSpec((spaces, n), lambda v: (0, first + v)),
            whole(),
        ],
        out_specs=pl.BlockSpec((n // 128, 128), lambda v: (v, 0)),
        out_shape=jax.ShapeDtypeStruct((pieces * n // 128, 128), F32),
        scratch_shapes=[
            pltpu.VMEM((n, width), BF16),
        ],
        compiler_params=params(),
        name="errors",
    )(rows, cent, codes, blocks)


def home_kernel(wide, owner_ref, rank_ref, first_ref, second_ref, out_ref):
    n = owner_ref.shape[1]
    rank = rank_ref[...]
    slot = (rank >> 4) * (wide * 16) + owner_ref[...] * 16 + (rank & 15)
    slot = jnp.where(rank < 0, -1, slot)
    left = jnp.concatenate([first_ref[...], second_ref[...]], axis=0)
    rows = left.shape[0]
    at_row = jnp.where(iota((rows, n), 0) == slot >> 7, 1.0, 0.0).astype(BF16)
    at_row = jnp.concatenate([at_row] * 3, axis=0)
    one = eye(128)
    pieces = []
    for _ in range(3):
        piece = left.astype(BF16)
        left = left - piece.astype(F32)
        pieces.append(dot_nt(one, piece))
    pieces = jnp.concatenate(pieces, axis=1).astype(BF16)
    slots = jnp.dot(pieces, at_row, preferred_element_type=F32)
    mine = iota((128, n), 0) == slot & 127
    out_ref[...] = jnp.sum(jnp.where(mine, slots, 0.0), axis=0, keepdims=True)


def bring_home(owner, rank, first, second, wide):
    n = owner.shape[1]
    return pl.pallas_call(
        functools.partial(home_kernel, wide),
        in_specs=[whole()] * 4,
        out_specs=whole(),
        out_shape=jax.ShapeDtypeStruct((1, n), F32),
        compiler_params=params(),
        name="bring_home",
    )(owner, rank, first, second)


def exchange(x):
    return lax.all_to_all(x, "wide", split_axis=0, concat_axis=0, tiled=True)


def swap_cores(x):
    return lax.ppermute(x, "narrow", [(0, 1), (1, 0)])


AXES = (4, 2)
LAST = 0


def along(axis):
    return (lax.axis_index("wide") >> axis) & 3


def swap_along(x, axis, d):
    return lax.ppermute(x, "wide", [(i, i ^ (d << axis)) for i in range(lax.axis_size("wide"))])


def part(x, i):
    return lax.dynamic_index_in_dim(x, i, 0, keepdims=False)


def reduce_cores(x):
    x = x.reshape((2, x.shape[0] // 2) + x.shape[1:])
    here = lax.axis_index("narrow")
    return part(x, here) + swap_cores(part(x, 1 - here))


def reduce_chips(x):
    for axis in AXES:
        x = x.reshape((4, x.shape[0] // 4) + x.shape[1:])
        here = along(axis)
        got = [swap_along(part(x, here ^ d), axis, d) for d in (1, 2, 3)]
        x = (part(x, here) + got[0]) + (got[1] + got[2])
    got = [swap_along(x, LAST, d) for d in (1, 2, 3)]
    return (x + got[0]) + (got[1] + got[2])


def spread_axis(x, axis):
    here = along(axis)
    got = [x]
    for d in (1, 2, 3):
        got.append(swap_along(x, axis, d))
    odd = (here & 1) == 1
    got = [jnp.where(odd, got[i ^ 1], got[i]) for i in range(4)]
    high = (here & 2) == 2
    got = [jnp.where(high, got[i ^ 2], got[i]) for i in range(4)]
    return jnp.concatenate(got, axis=0)


def spread_cores(x):
    other = swap_cores(x)
    first = lax.axis_index("narrow") == 0
    return jnp.concatenate([jnp.where(first, x, other), jnp.where(first, other, x)], axis=0)


def own_share():
    share = lax.axis_index("narrow")
    for axis in AXES:
        share = share * 4 + along(axis)
    return share


def refit_step(rows, list_ids, codes, row_counts, centroids, old_codebook):
    local_rows, width = rows.shape
    spaces = codes.shape[1]
    wide = lax.axis_size("wide")
    cap = 2 * local_rows // wide
    first = 64
    lists = centroids.shape[0]
    assert width // 128 == 8
    own = lax.axis_index("wide")
    anchor = float(local_rows * lax.axis_size("narrow") * wide // (4 * K))

    def pieces(x):
        return x.reshape(wide, -1, 16, width)

    owner, rank, src, scaled, lst = route(list_ids, row_counts, wide, lists)
    sent_codes, codes_local = pick_codes(codes, src, lst, row_counts, cap)
    got_codes = exchange(sent_codes)
    rows_slots = pieces(pick(rows, scaled, 0, cap))
    codes_here = turn(sent_codes)
    got_lists = lists_of(got_codes, width // 128)
    cent_first = pick(centroids, got_lists, 0, first)
    got_first = pieces(exchange(cent_first))
    cent_second = pick(centroids, got_lists, first, cap - first)

    codes_there = turn(got_codes)
    sums = gram(rows.reshape(-1, 1, 16, width), codes_local)
    sums, rows_slots = lax.optimization_barrier((sums, rows_slots))
    sums = gram(pieces(cent_first), codes_there, 0, sums)
    sums = gram(pieces(cent_second), codes_there, first // (cap - first), sums)
    mine = reduce_cores(sums)
    mine = reduce_chips(mine)
    share = mine.shape[0]
    old = lax.dynamic_slice_in_dim(old_codebook, own_share() * share, share, 0).reshape(share, K * SUB // 128, 128)
    book = refit(mine, old, anchor)
    for axis in reversed(AXES):
        book = spread_axis(book, axis)
    cent_second, book = lax.optimization_barrier((cent_second, book))
    book = spread_cores(book)
    got_second = pieces(exchange(cent_second))
    codebook = book.reshape(spaces, K * SUB)
    search_table = lax.dynamic_slice_in_dim(codebook, own, 1, 0).astype(BF16)

    blocks = tiles(book)
    err_first = errors(rows_slots, got_first, codes_here, blocks, 0)
    err_second = errors(rows_slots, got_second, codes_here, blocks, first // 16)
    row_error = bring_home(owner, rank, err_first, err_second, wide).reshape(local_rows)
    return (codebook, search_table, row_error)


def solution(mesh):
    in_specs = (
        P(("narrow", "wide"), None),
        P(("narrow", "wide")),
        P(("narrow", "wide"), None),
        P(("narrow", "wide")),
        P("wide", None),
        P(),
    )
    out_specs = (P(), P("wide", None), P(("narrow", "wide")))
    return jax.shard_map(refit_step, mesh=mesh, in_specs=in_specs, out_specs=out_specs, check_vma=False)
```
